256 devices in a mesh: lat: 4 (over x_lo, core), lon: 64 (over x_hi, z, y).
Axes of the slice: x: 4 (x_hi: 2, x_lo: 2; x = x_hi * 2 + x_lo), y: 4, z: 8, core: 2. Of those that a mesh axis runs over, the one named last changes fastest.
Arguments:
- adjoint_in: float32 [16, 3, 136, 8192], P('lat', None, None, 'lon'), may hold values from -6 to 6
- frac_x: float32 [16, 8192], P('lat', 'lon'), may hold values from 0 to 1
- frac_y: float32 [16, 8192], P('lat', 'lon'), may hold values from 0 to 1
- dep_tile: int32 [16], P('lat'), may hold values from -1 to 0, as said below
- dep_col: int32 [16], P('lat'), may hold values from 0 to 127
- block_inverse: float32 [16, 2, 68, 68], P('lat'), may hold values from -0.25 to 1
- coupling: float32 [16, 8192], P('lat', 'lon'), may hold values from 0.15 to 0.6
Outputs:
- adjoint_out: float32 [16, 3, 136, 8192], P('lat', None, None, 'lon')
The draws below stay inside these ranges and needn't reach their ends.
Inputs may be any that keep to these rules, and one draw needn't show every extreme that they name: dep_tile * 128 + dep_col is the row's departure offset in columns; it equals -128 in some row and 127 in another.
All inputs are finite; a program needn't handle non-finite values.
Results may differ from the reference program's by a relative error of at most 0.0003.
Values sent between devices are 32-bit elements; how exact they have to be, the bound alone decides.
A program may use at most 64 MiB of HBM per device.

```python
import jax
import jax.numpy as jnp
from jax import lax

TRACERS = 3
LEV = 136
BLOCK = 68
REACH = 1
COLS = 128
NBLK = 2
NLAT = 16
NLON = 8192


def departure_offsets(key):
    offset_limit = REACH * COLS
    drawn_offsets = jax.random.randint(jax.random.fold_in(key, 11), (NLAT,), -offset_limit, offset_limit, dtype=jnp.int32)
    row_order = jax.random.permutation(jax.random.fold_in(key, 12), NLAT)
    drawn_offsets = drawn_offsets.at[row_order[0]].set(-offset_limit)
    drawn_offsets = drawn_offsets.at[row_order[1]].set(offset_limit - 1)
    return drawn_offsets


def draw_dep_tile(key, part):
    return jnp.floor_divide(departure_offsets(key), COLS).astype(jnp.int32)


def draw_dep_col(key, part):
    drawn_offsets = departure_offsets(key)
    return (drawn_offsets - jnp.floor_divide(drawn_offsets, COLS) * COLS).astype(jnp.int32)


def draw_block_inverse(key, part):
    diagonal = jax.random.uniform(jax.random.fold_in(key, 21), (NLAT, NBLK, BLOCK, 1), jnp.float32, 0.5, 1.0)
    spread = jax.random.uniform(jax.random.fold_in(key, 22), (NLAT, NBLK, BLOCK, BLOCK), jnp.float32, -0.25, 0.25)
    on_diagonal = lax.broadcasted_iota(jnp.int32, (NLAT, NBLK, BLOCK, BLOCK), 2) == lax.broadcasted_iota(jnp.int32, (NLAT, NBLK, BLOCK, BLOCK), 3)
    return jnp.where(on_diagonal, diagonal, spread).astype(jnp.float32)


def steps_of(rng, shape, shards, smallest, largest):
    def one(position, shards_of):
        draws = jax.random.uniform(jax.random.fold_in(jax.random.fold_in(rng, 6), position), (shards_of,), jnp.float32, smallest / len(shards), largest / len(shards))
        return jnp.repeat(jnp.exp(draws), shape[position] // shards_of).reshape((-1,) + (1,) * (len(shape) - position - 1))

    loudness = one(*shards[0])
    for cut in shards[1:]:
        loudness = loudness * one(*cut)
    return loudness


def scatter_about(key, extent, width, bound, cuts=(), kind=jnp.bfloat16):
    drawn = jax.random.normal(key, extent, jnp.float32) * width
    if len(cuts) > 0:
        drawn = steps_of(key, extent, cuts, -0.22, 0.18) * drawn
    return jnp.clip(drawn, min=-bound, max=bound).astype(kind)


def setup_inputs(seed: int = 0) -> dict:
    streams_of = jax.random.split(jax.random.key(seed), 8)
    adjoint_in = scatter_about(streams_of[0], (NLAT, TRACERS, LEV, NLON), 1.0, 6.0, ((0, 4), (3, 64)), jnp.float32)
    frac_x = jnp.clip(1.0 * jax.random.uniform(streams_of[1], (NLAT, NLON), jnp.float32) ** steps_of(streams_of[1], (NLAT, NLON), ((0, 4), (1, 64)), -0.2, 0.2), 0.0, 1.0)
    frac_y = jnp.clip(1.0 * jax.random.uniform(streams_of[2], (NLAT, NLON), jnp.float32) ** steps_of(streams_of[2], (NLAT, NLON), ((0, 4), (1, 64)), -0.2, 0.2), 0.0, 1.0)
    dep_tile = draw_dep_tile(jax.random.fold_in(streams_of[7], 71), 0)
    dep_col = draw_dep_col(jax.random.fold_in(streams_of[7], 71), 0)
    block_inverse = draw_block_inverse(jax.random.fold_in(streams_of[7], 71), 0)
    coupling = jnp.clip(0.15 + 0.45000002 * jax.random.uniform(streams_of[6], (NLAT, NLON), jnp.float32) ** steps_of(streams_of[6], (NLAT, NLON), ((0, 4), (1, 64)), -0.2, 0.2), 0.15, 0.6)
    return dict(adjoint_in=adjoint_in, frac_x=frac_x, frac_y=frac_y, dep_tile=dep_tile, dep_col=dep_col, block_inverse=block_inverse, coupling=coupling)


def cubic_weights(fraction):
    plus_one = fraction + 1.0
    minus_one = fraction - 1.0
    minus_two = fraction - 2.0
    return jnp.stack([-fraction * minus_one * minus_two / 6.0, plus_one * minus_one * minus_two / 2.0, -plus_one * fraction * minus_two / 2.0, plus_one * fraction * minus_one / 6.0])


def vertical(field_in, inverse, coupling):
    row_count, tracer_count, level_count, col_count = field_in.shape
    block_count = inverse.shape[1]
    block_size = inverse.shape[2]
    blocks = field_in.reshape(row_count, tracer_count, block_count, block_size, col_count)
    first_sweep = jnp.einsum("rnij,rtnjc->rtnic", inverse, blocks, precision=lax.Precision.HIGHEST)
    coupling_now = coupling[:, None, None, :]
    adjusted = blocks.at[:, :, :-1, block_size - 1, :].add(coupling_now * first_sweep[:, :, 1:, 0, :])
    adjusted = adjusted.at[:, :, 1:, 0, :].add(coupling_now * first_sweep[:, :, :-1, block_size - 1, :])
    second_sweep = jnp.einsum("rnij,rtnjc->rtnic", inverse, adjusted, precision=lax.Precision.HIGHEST)
    return second_sweep.reshape(row_count, tracer_count, level_count, col_count)


def reference(adjoint_in, frac_x, frac_y, dep_tile, dep_col, block_inverse, coupling):
    lat_rows = adjoint_in.shape[0]
    shifts = dep_tile * COLS + dep_col
    weights_x = cubic_weights(frac_x)
    weights_y = cubic_weights(frac_y)

    def one_target(target):
        summed = jnp.zeros(adjoint_in.shape[1:], jnp.float32)
        for a in range(4):
            source = target - a + 1
            inside = jnp.where((source >= 0) & (source < lat_rows), 1.0, 0.0).astype(jnp.float32)
            source_row = jnp.clip(source, 0, lat_rows - 1).astype(jnp.int32)
            values = adjoint_in[source_row]
            for b in range(4):
                factor = weights_y[a, source_row] * weights_x[b, source_row]
                summed = summed + inside * jnp.roll(factor * values, shifts[source_row] + b - 1, axis=2)
        return vertical(summed[None], block_inverse[target][None], coupling[target][None])[0]

    return lax.map(one_target, jnp.arange(lat_rows, dtype=jnp.int32))
```

```python
import jax
import jax.numpy as jnp
from jax import lax
from jax.experimental import pallas as pl
from jax.experimental.pallas import tpu as pltpu
from jax.sharding import PartitionSpec as P

MESH = pl.DeviceIdType.MESH
ORDER = [(3, 0), (2, 0), (3, 1), (2, 1), (3, 2), (2, 2), (0, 0), (0, 1), (0, 2), (1, 0), (1, 1), (1, 2)]
HEAD = 6


def cubic(f):
    p, m1, m2 = f + 1.0, f - 1.0, f - 2.0
    sixth = 1.0 / 6.0
    return (-f * m1 * m2 * sixth, p * m1 * m2 * 0.5, -p * f * m2 * 0.5, p * f * m1 * sixth)


def kernel(
    tile_ref, col_ref, x_hbm, fx_ref, fy_ref, inv_ref, cpl_ref, out_ref,
    own, left, right, acc, from_prev, from_next, fxl, fxr, fyl, fyr,
    edge_r, edge_l, hop_l, hop_r, far_l, far_r, weights, ahi, alo, bcol,
    own_sem, send_sem, recv_sem, fsend, frecv, esend, erecv, lsend, lrecv,
):
    rows, tracers, levels, cols = x_hbm.shape
    half = levels // 2
    nlon, nlat = lax.axis_size("lon"), lax.axis_size("lat")
    lon, lat = lax.axis_index("lon"), lax.axis_index("lat")
    to_right = (lat, lax.rem(lon + 1, nlon))
    to_left = (lat, lax.rem(lon + nlon - 1, nlon))
    has_prev, has_next = lat > 0, lat < nlat - 1

    barrier = pltpu.get_barrier_semaphore()
    pl.semaphore_signal(barrier, inc=1, device_id=to_right, device_id_type=MESH)
    pl.semaphore_signal(barrier, inc=1, device_id=to_left, device_id_type=MESH)

    @pl.when(has_prev)
    def _():
        pl.semaphore_signal(barrier, inc=1, device_id=(lat - 1, lon), device_id_type=MESH)

    @pl.when(has_next)
    def _():
        pl.semaphore_signal(barrier, inc=1, device_id=(lat + 1, lon), device_id_type=MESH)

    own_copy = pltpu.make_async_copy(x_hbm, own, own_sem)
    own_copy.start()

    def remote(src, dst, ss, rs, to):
        return pltpu.make_async_remote_copy(src, dst, ss, rs, device_id=to, device_id_type=MESH)

    pl.semaphore_wait(barrier, 2 + has_prev.astype(jnp.int32) + has_next.astype(jnp.int32))

    small = [
        remote(fx_ref, fxl, fsend.at[0], frecv.at[0], to_right),
        remote(fy_ref, fyl, fsend.at[1], frecv.at[1], to_right),
        remote(fx_ref, fxr, fsend.at[2], frecv.at[2], to_left),
        remote(fy_ref, fyr, fsend.at[3], frecv.at[3], to_left),
    ]
    for copy in small:
        copy.start()
    big = []
    for k, (r, t) in enumerate(ORDER):
        big.append((
            remote(x_hbm.at[r, t], left.at[k], send_sem.at[0, k], recv_sem.at[0, k], to_right),
            remote(x_hbm.at[r, t], right.at[k], send_sem.at[1, k], recv_sem.at[1, k], to_left),
        ))
    for a, b in big[:HEAD]:
        a.start()
        b.start()

    own_copy.wait()
    eye = lax.broadcasted_iota(jnp.int32, (cols, cols), 0) == lax.broadcasted_iota(jnp.int32, (cols, cols), 1)
    rest = levels - cols
    eye_rest = lax.broadcasted_iota(jnp.int32, (rest, cols), 0) == lax.broadcasted_iota(jnp.int32, (rest, cols), 1)
    for r in range(rows):
        for t in range(tracers):
            k = r * tracers + t
            for lane, edge in ((cols - 1, edge_r), (0, edge_l)):
                column = jnp.broadcast_to(own[r, t, :, lane : lane + 1], (levels, cols))
                edge[k : k + 1, 0:cols] = jnp.sum(jnp.where(eye, column[:cols], 0.0), axis=0, keepdims=True)
                edge[k : k + 1, cols : 2 * cols] = jnp.sum(jnp.where(eye_rest, column[cols:], 0.0), axis=0, keepdims=True)
    base = rows * tracers
    for lane, edge in ((cols - 1, edge_r), (0, edge_l)):
        edge[base : base + rows, 0:cols] = jnp.broadcast_to(fx_ref[:, lane : lane + 1], (rows, cols))
        edge[base : base + rows, cols : 2 * cols] = jnp.broadcast_to(fy_ref[:, lane : lane + 1], (rows, cols))

    sub = lax.broadcasted_iota(jnp.int32, (levels, cols), 0)
    for r in range(rows):
        top = jnp.concatenate([inv_ref[r, 0], jnp.zeros((half, half), jnp.float32)], axis=1)
        low = jnp.concatenate([jnp.zeros((half, half), jnp.float32), inv_ref[r, 1]], axis=1)
        whole = jnp.concatenate([top, low], axis=0)
        hi = whole.astype(jnp.bfloat16)
        ahi[r] = hi
        alo[r] = (whole - hi.astype(jnp.float32)).astype(jnp.bfloat16)
        column = jnp.concatenate([inv_ref[r, 0, :, half - 1 : half], inv_ref[r, 1, :, 0:1]], axis=0)
        bcol[r] = jnp.broadcast_to(column, (levels, cols))

    edge_copies = [
        remote(edge_r, hop_l, esend.at[0], erecv.at[0], to_right),
        remote(edge_l, hop_r, esend.at[1], erecv.at[1], to_left),
        remote(hop_l, far_l, esend.at[2], erecv.at[2], to_right),
        remote(hop_r, far_r, esend.at[3], erecv.at[3], to_left),
    ]
    edge_copies[0].start()
    edge_copies[1].start()
    edge_copies[0].wait_recv()
    edge_copies[2].start()
    edge_copies[1].wait_recv()
    edge_copies[3].start()
    for a, b in big[HEAD:]:
        a.start()
        b.start()

    for copy in small:
        copy.wait_recv()
    edge_copies[2].wait_recv()
    edge_copies[3].wait_recv()

    lane = lax.broadcasted_iota(jnp.int32, (8, cols), 1)
    shifts = [tile_ref[r] * cols + col_ref[r] for r in range(rows)]

    def sources(s, b):
        d = s + (b - 1)
        return lax.shift_right_arithmetic(lane + d, 7), jnp.bitwise_and(d, cols - 1)

    def vec(ref, r, c0=0):
        return jnp.broadcast_to(ref[r : r + 1, c0 : c0 + cols], (8, cols))

    for r in range(rows):
        s = shifts[r]
        fx3 = (vec(fx_ref, r), vec(fxl, r), vec(fxr, r))
        fy3 = (vec(fy_ref, r), vec(fyl, r), vec(fyr, r))
        for b in range(4):
            where, turn = sources(s, b)
            shifted = []
            for (here, l, rt), c0 in ((fx3, 0), (fy3, cols)):
                v = jnp.where(where > 0, l, jnp.where(where < 0, rt, here))
                if b == 3:
                    v = jnp.where(where == 2, vec(far_l, base + r, c0), v)
                if b == 0:
                    v = jnp.where(where == -2, vec(far_r, base + r, c0), v)
                shifted.append(pltpu.roll(v, turn, 1))
            wx = cubic(shifted[0])[b]
            for a, wy in enumerate(cubic(shifted[1])):
                weights[r, a * 4 + b] = wx * wy

    lane8 = lane - lax.broadcasted_iota(jnp.int32, (8, cols), 0)

    def spread(k, r, t):
        s = shifts[r]
        sv = jnp.full((8, cols), 0, jnp.int32) + s
        lo_right, hi_left = sv <= 0, sv >= -1
        src = [sources(s, b) for b in range(4)]
        g = [[weights[r, a * 4 + b] for b in range(4)] for a in range(4)]
        kk = r * tracers + t
        for i in range(levels // 8):
            rs = slice(8 * i, 8 * i + 8)
            here, l, rt = own[r, t, rs, :], left[k, rs, :], right[k, rs, :]
            c0 = cols * ((8 * i) // cols)
            far = jnp.where(hi_left, vec(far_l, kk, c0), vec(far_r, kk, c0))
            far = jnp.sum(jnp.where(lane8 == (8 * i) % cols, far, 0.0), axis=1, keepdims=True)
            far = jnp.broadcast_to(far, (8, cols))
            near_lo, near_hi = jnp.where(lo_right, rt, l), jnp.where(hi_left, l, rt)
            u = []
            for b in range(4):
                where, turn = src[b]
                v = jnp.where(where == 0, here, near_lo if b < 2 else near_hi)
                if b == 3:
                    v = jnp.where(where == 2, far, v)
                if b == 0:
                    v = jnp.where(where == -2, far, v)
                u.append(pltpu.roll(v, turn, 1))
            for a in range(4):
                part = (g[a][0] * u[0] + g[a][1] * u[1]) + (g[a][2] * u[2] + g[a][3] * u[3])
                first = r == 3 or (r == 2 and a == 0) or (r == 0 and a < 2)
                acc[t, r + a, rs, :] = part if first else acc[t, r + a, rs, :] + part

    def next_copy(t):
        return remote(acc.at[t, pl.ds(rows + 1, 2)], from_prev.at[t], lsend.at[0, t], lrecv.at[0, t], (lat + 1, lon))

    def prev_copy(t):
        return remote(acc.at[t, 0], from_next.at[t], lsend.at[1, t], lrecv.at[1, t], (lat - 1, lon))

    def final(t):
        @pl.when(has_prev)
        def _():
            next_copy(t).wait_recv()

        @pl.when(has_next)
        def _():
            prev_copy(t).wait_recv()

        for i in range(rows):
            x = acc[t, i + 1]
            if i < 2:
                x = x + from_prev[t, i]
            if i == rows - 1:
                x = x + from_next[t]
            hi = x.astype(jnp.bfloat16)
            lo = (x - hi.astype(jnp.float32)).astype(jnp.bfloat16)
            p = jnp.dot(ahi[i], hi, preferred_element_type=jnp.float32)
            p = p + jnp.dot(ahi[i], lo, preferred_element_type=jnp.float32)
            p = p + jnp.dot(alo[i], hi, preferred_element_type=jnp.float32)
            c = cpl_ref[i : i + 1, :]
            above = jnp.broadcast_to(c * p[half : half + 1], (levels, cols))
            below = jnp.broadcast_to(c * p[half - 1 : half], (levels, cols))
            out_ref[i, t] = p + bcol[i] * jnp.where(sub < half, above, below)

    @pl.when(jnp.logical_not(has_prev))
    def _():
        from_prev[...] = jnp.zeros_like(from_prev)

    @pl.when(jnp.logical_not(has_next))
    def _():
        from_next[...] = jnp.zeros_like(from_next)

    due = []
    for k, (r, t) in enumerate(ORDER):
        big[k][0].wait_recv()
        big[k][1].wait_recv()
        spread(k, r, t)
        for send in due:
            send()
        due = []
        if r == 2:
            def send(t=t):
                @pl.when(has_next)
                def _():
                    next_copy(t).start()
            due.append(send)
        if r == 0:
            def send(t=t):
                @pl.when(has_prev)
                def _():
                    prev_copy(t).start()
            due.append(send)
        if r == 1:
            final(t)

    for copy in small + edge_copies:
        copy.wait_send()
    for a, b in big:
        a.wait_send()
        b.wait_send()

    @pl.when(has_next)
    def _():
        for t in range(tracers):
            next_copy(t).wait_send()

    @pl.when(has_prev)
    def _():
        for t in range(tracers):
            prev_copy(t).wait_send()


def on_device(adjoint_in, frac_x, frac_y, dep_tile, dep_col, block_inverse, coupling):
    rows, tracers, levels, cols = adjoint_in.shape
    blocks = rows * tracers
    f32, dma = jnp.float32, pltpu.SemaphoreType.DMA
    vmem, smem = pl.BlockSpec(memory_space=pltpu.VMEM), pl.BlockSpec(memory_space=pltpu.SMEM)
    return pl.pallas_call(
        kernel,
        out_shape=jax.ShapeDtypeStruct(adjoint_in.shape, f32),
        in_specs=[smem, smem, pl.BlockSpec(memory_space=pl.ANY), vmem, vmem, vmem, vmem],
        out_specs=vmem,
        scratch_shapes=[
            pltpu.VMEM((rows, tracers, levels, cols), f32),
            pltpu.VMEM((blocks, levels, cols), f32),
            pltpu.VMEM((blocks, levels, cols), f32),
            pltpu.VMEM((tracers, rows + 3, levels, cols), f32),
            pltpu.VMEM((tracers, 2, levels, cols), f32),
            pltpu.VMEM((tracers, levels, cols), f32),
            *[pltpu.VMEM((rows, cols), f32)] * 4,
            *[pltpu.VMEM((blocks + rows, 2 * cols), f32)] * 6,
            pltpu.VMEM((rows, 16, 8, cols), f32),
            pltpu.VMEM((rows, levels, levels), jnp.bfloat16),
            pltpu.VMEM((rows, levels, levels), jnp.bfloat16),
            pltpu.VMEM((rows, levels, cols), f32),
            dma,
            dma((2, blocks)),
            dma((2, blocks)),
            dma((4,)),
            dma((4,)),
            dma((4,)),
            dma((4,)),
            dma((2, tracers)),
            dma((2, tracers)),
        ],
        compiler_params=pltpu.CompilerParams(collective_id=0, has_side_effects=True),
    )(dep_tile, dep_col, adjoint_in, frac_x, frac_y, block_inverse, coupling)


def solution(mesh):
    return jax.shard_map(
        on_device,
        mesh=mesh,
        in_specs=(
            P("lat", None, None, "lon"),
            P("lat", "lon"),
            P("lat", "lon"),
            P("lat"),
            P("lat"),
            P("lat", None, None, None),
            P("lat", "lon"),
        ),
        out_specs=P("lat", None, None, "lon"),
        check_vma=False,
    )
```

```python
import jax
import jax.numpy as jnp
from jax import lax
from jax.experimental import pallas as pl
from jax.experimental.pallas import tpu as pltpu
from jax.sharding import PartitionSpec as P

MESH = pl.DeviceIdType.MESH
ORDER = [(3, 0), (2, 0), (3, 1), (2, 1), (3, 2), (2, 2), (0, 0), (0, 1), (0, 2), (1, 0), (1, 1), (1, 2)]
HEAD, HEAD2 = 2, 4


def cubic(f):
    p, m1, m2 = f + 1.0, f - 1.0, f - 2.0
    sixth = 1.0 / 6.0
    return (-f * m1 * m2 * sixth, p * m1 * m2 * 0.5, -p * f * m2 * 0.5, p * f * m1 * sixth)


def kernel(
    tile_hbm, col_hbm, x_hbm, fx_hbm, fy_hbm, inv_hbm, cpl_hbm, out_ref,
    tile_ref, col_ref, fx_ref, fy_ref, inv_ref, cpl_ref, own, left, right, acc, from_prev, from_next, fxl, fxr, fyl, fyr,
    edge_r, edge_l, hop_l, hop_r, far_l, far_r, weights, ahi, alo, bcol,
    own_sem, in_sem, send_sem, recv_sem, fsend, frecv, esend, erecv, lsend, lrecv,
):
    rows, tracers, levels, cols = x_hbm.shape
    half = levels // 2
    nlon, nlat = lax.axis_size("lon"), lax.axis_size("lat")
    lon, lat = lax.axis_index("lon"), lax.axis_index("lat")
    to_right = (lat, lax.rem(lon + 1, nlon))
    to_left = (lat, lax.rem(lon + nlon - 1, nlon))
    has_prev, has_next = lat > 0, lat < nlat - 1

    barrier = pltpu.get_barrier_semaphore()
    pl.semaphore_signal(barrier, inc=1, device_id=to_right, device_id_type=MESH)
    pl.semaphore_signal(barrier, inc=1, device_id=to_left, device_id_type=MESH)

    @pl.when(has_prev)
    def _():
        pl.semaphore_signal(barrier, inc=1, device_id=(lat - 1, lon), device_id_type=MESH)

    @pl.when(has_next)
    def _():
        pl.semaphore_signal(barrier, inc=1, device_id=(lat + 1, lon), device_id_type=MESH)

    def remote(src, dst, ss, rs, to):
        return pltpu.make_async_remote_copy(src, dst, ss, rs, device_id=to, device_id_type=MESH)

    pl.semaphore_wait(barrier, 2 + has_prev.astype(jnp.int32) + has_next.astype(jnp.int32))

    edge_copies = [
        remote(edge_r, hop_l, esend.at[0], erecv.at[0], to_right),
        remote(edge_l, hop_r, esend.at[1], erecv.at[1], to_left),
        remote(hop_l, far_l, esend.at[2], erecv.at[2], to_right),
        remote(hop_r, far_r, esend.at[3], erecv.at[3], to_left),
    ]
    small = [
        remote(fx_hbm, fxl, fsend.at[0], frecv.at[0], to_right),
        remote(fy_hbm, fyl, fsend.at[1], frecv.at[1], to_right),
        remote(fx_hbm, fxr, fsend.at[2], frecv.at[2], to_left),
        remote(fy_hbm, fyr, fsend.at[3], frecv.at[3], to_left),
    ]
    big = []
    for k, (r, t) in enumerate(ORDER):
        big.append((
            remote(x_hbm.at[r, t], left.at[k], send_sem.at[0, k], recv_sem.at[0, k], to_right),
            remote(x_hbm.at[r, t], right.at[k], send_sem.at[1, k], recv_sem.at[1, k], to_left),
        ))
    for a, b in big[:HEAD]:
        a.start()
        b.start()
    for copy in small:
        copy.start()
    own_copy = pltpu.make_async_copy(x_hbm, own, own_sem)
    own_copy.start()
    loads = [
        pltpu.make_async_copy(src, dst, in_sem.at[i])
        for i, (src, dst) in enumerate((
            (fx_hbm, fx_ref), (fy_hbm, fy_ref), (tile_hbm, tile_ref),
            (col_hbm, col_ref), (cpl_hbm, cpl_ref), (inv_hbm, inv_ref),
        ))
    ]
    for copy in loads:
        copy.start()
    for copy in loads[:2]:
        copy.wait()

    own_copy.wait()
    eye = lax.broadcasted_iota(jnp.int32, (cols, cols), 0) == lax.broadcasted_iota(jnp.int32, (cols, cols), 1)
    rest = levels - cols
    eye_rest = lax.broadcasted_iota(jnp.int32, (rest, cols), 0) == lax.broadcasted_iota(jnp.int32, (rest, cols), 1)
    for r in range(rows):
        for t in range(tracers):
            k = r * tracers + t
            for lane, edge in ((cols - 1, edge_r), (0, edge_l)):
                column = jnp.broadcast_to(own[r, t, :, lane : lane + 1], (levels, cols))
                edge[k : k + 1, 0:cols] = jnp.sum(jnp.where(eye, column[:cols], 0.0), axis=0, keepdims=True)
                edge[k : k + 1, cols : 2 * cols] = jnp.sum(jnp.where(eye_rest, column[cols:], 0.0), axis=0, keepdims=True)
    base = rows * tracers
    for lane, edge in ((cols - 1, edge_r), (0, edge_l)):
        edge[base : base + rows, 0:cols] = jnp.broadcast_to(fx_ref[:, lane : lane + 1], (rows, cols))
        edge[base : base + rows, cols : 2 * cols] = jnp.broadcast_to(fy_ref[:, lane : lane + 1], (rows, cols))

    edge_copies[0].start()
    edge_copies[1].start()
    for a, b in big[HEAD:HEAD2]:
        a.start()
        b.start()
    for copy in loads[2:]:
        copy.wait()

    edge_copies[0].wait_recv()
    edge_copies[2].start()
    edge_copies[1].wait_recv()
    edge_copies[3].start()
    for a, b in big[HEAD2:]:
        a.start()
        b.start()

    sub = lax.broadcasted_iota(jnp.int32, (levels, cols), 0)
    for r in range(rows):
        top = jnp.concatenate([inv_ref[r, :, 0, :], jnp.zeros((half, half), jnp.float32)], axis=1)
        low = jnp.concatenate([jnp.zeros((half, half), jnp.float32), inv_ref[r, :, 1, :]], axis=1)
        whole = jnp.concatenate([top, low], axis=0)
        hi = whole.astype(jnp.bfloat16)
        ahi[r] = hi
        alo[r] = (whole - hi.astype(jnp.float32)).astype(jnp.bfloat16)
        column = jnp.concatenate([inv_ref[r, :, 0, half - 1 : half], inv_ref[r, :, 1, 0:1]], axis=0)
        bcol[r] = jnp.broadcast_to(column, (levels, cols))

    for copy in small:
        copy.wait_recv()
    edge_copies[2].wait_recv()
    edge_copies[3].wait_recv()

    lane = lax.broadcasted_iota(jnp.int32, (8, cols), 1)
    shifts = [tile_ref[r] * cols + col_ref[r] for r in range(rows)]

    def sources(s, b):
        d = s + (b - 1)
        return lax.shift_right_arithmetic(lane + d, 7), jnp.bitwise_and(d, cols - 1)

    def vec(ref, r, c0=0):
        return jnp.broadcast_to(ref[r : r + 1, c0 : c0 + cols], (8, cols))

    for r in range(rows):
        s = shifts[r]
        fx3 = (vec(fx_ref, r), vec(fxl, r), vec(fxr, r))
        fy3 = (vec(fy_ref, r), vec(fyl, r), vec(fyr, r))
        for b in range(4):
            where, turn = sources(s, b)
            shifted = []
            for (here, l, rt), c0 in ((fx3, 0), (fy3, cols)):
                v = jnp.where(where > 0, l, jnp.where(where < 0, rt, here))
                if b == 3:
                    v = jnp.where(where == 2, vec(far_l, base + r, c0), v)
                if b == 0:
                    v = jnp.where(where == -2, vec(far_r, base + r, c0), v)
                shifted.append(pltpu.roll(v, turn, 1))
            wx = cubic(shifted[0])[b]
            for a, wy in enumerate(cubic(shifted[1])):
                weights[r, a * 4 + b] = wx * wy

    lane8 = lane - lax.broadcasted_iota(jnp.int32, (8, cols), 0)

    def spread(k, r, t):
        s = shifts[r]
        sv = jnp.full((8, cols), 0, jnp.int32) + s
        lo_right, hi_left = sv <= 0, sv >= -1
        src = [sources(s, b) for b in range(4)]
        g = [[weights[r, a * 4 + b] for b in range(4)] for a in range(4)]
        kk = r * tracers + t
        for i in range(levels // 8):
            rs = slice(8 * i, 8 * i + 8)
            here, l, rt = own[r, t, rs, :], left[k, rs, :], right[k, rs, :]
            c0 = cols * ((8 * i) // cols)
            far = jnp.where(hi_left, vec(far_l, kk, c0), vec(far_r, kk, c0))
            far = jnp.sum(jnp.where(lane8 == (8 * i) % cols, far, 0.0), axis=1, keepdims=True)
            far = jnp.broadcast_to(far, (8, cols))
            near_lo, near_hi = jnp.where(lo_right, rt, l), jnp.where(hi_left, l, rt)
            u = []
            for b in range(4):
                where, turn = src[b]
                v = jnp.where(where == 0, here, near_lo if b < 2 else near_hi)
                if b == 3:
                    v = jnp.where(where == 2, far, v)
                if b == 0:
                    v = jnp.where(where == -2, far, v)
                u.append(pltpu.roll(v, turn, 1))
            for a in range(4):
                part = (g[a][0] * u[0] + g[a][1] * u[1]) + (g[a][2] * u[2] + g[a][3] * u[3])
                first = r == 3 or (r == 2 and a == 0) or (r == 0 and a < 2)
                acc[t, r + a, rs, :] = part if first else acc[t, r + a, rs, :] + part

    def next_copy(t):
        return remote(acc.at[t, pl.ds(rows + 1, 2)], from_prev.at[t], lsend.at[0, t], lrecv.at[0, t], (lat + 1, lon))

    def prev_copy(t):
        return remote(acc.at[t, 0], from_next.at[t], lsend.at[1, t], lrecv.at[1, t], (lat - 1, lon))

    def final(t):
        @pl.when(has_prev)
        def _():
            next_copy(t).wait_recv()

        @pl.when(has_next)
        def _():
            prev_copy(t).wait_recv()

        for i in range(rows):
            x = acc[t, i + 1]
            if i < 2:
                x = x + from_prev[t, i]
            if i == rows - 1:
                x = x + from_next[t]
            hi = x.astype(jnp.bfloat16)
            lo = (x - hi.astype(jnp.float32)).astype(jnp.bfloat16)
            p = jnp.dot(ahi[i], hi, preferred_element_type=jnp.float32)
            p = p + jnp.dot(ahi[i], lo, preferred_element_type=jnp.float32)
            p = p + jnp.dot(alo[i], hi, preferred_element_type=jnp.float32)
            c = cpl_ref[i : i + 1, :]
            above = jnp.broadcast_to(c * p[half : half + 1], (levels, cols))
            below = jnp.broadcast_to(c * p[half - 1 : half], (levels, cols))
            out_ref[i, t] = p + bcol[i] * jnp.where(sub < half, above, below)

    @pl.when(jnp.logical_not(has_prev))
    def _():
        from_prev[...] = jnp.zeros_like(from_prev)

    @pl.when(jnp.logical_not(has_next))
    def _():
        from_next[...] = jnp.zeros_like(from_next)

    for k, (r, t) in enumerate(ORDER):
        big[k][0].wait_recv()
        big[k][1].wait_recv()
        spread(k, r, t)
        if r == 2:
            @pl.when(has_next)
            def _(t=t):
                next_copy(t).start()

        if r == 0:
            @pl.when(has_prev)
            def _(t=t):
                prev_copy(t).start()

        if r == 1:
            final(t)

    for copy in small + edge_copies:
        copy.wait_send()
    for a, b in big:
        a.wait_send()
        b.wait_send()

    @pl.when(has_next)
    def _():
        for t in range(tracers):
            next_copy(t).wait_send()

    @pl.when(has_prev)
    def _():
        for t in range(tracers):
            prev_copy(t).wait_send()


def on_device(adjoint_in, frac_x, frac_y, dep_tile, dep_col, block_inverse, coupling):
    rows, tracers, levels, cols = adjoint_in.shape
    blocks = rows * tracers
    f32, dma = jnp.float32, pltpu.SemaphoreType.DMA
    return pl.pallas_call(
        kernel,
        out_shape=pltpu.VMEM(adjoint_in.shape, f32),
        in_specs=[pl.BlockSpec(memory_space=pl.ANY)] * 7,
        out_specs=pl.BlockSpec(memory_space=pltpu.VMEM),
        scratch_shapes=[
            pltpu.SMEM(dep_tile.shape, jnp.int32),
            pltpu.SMEM(dep_col.shape, jnp.int32),
            pltpu.VMEM((rows, cols), f32),
            pltpu.VMEM((rows, cols), f32),
            pltpu.VMEM((rows, levels // 2, 2, levels // 2), f32),
            pltpu.VMEM((rows, cols), f32),
            pltpu.VMEM((rows, tracers, levels, cols), f32),
            pltpu.VMEM((blocks, levels, cols), f32),
            pltpu.VMEM((blocks, levels, cols), f32),
            pltpu.VMEM((tracers, rows + 3, levels, cols), f32),
            pltpu.VMEM((tracers, 2, levels, cols), f32),
            pltpu.VMEM((tracers, levels, cols), f32),
            *[pltpu.VMEM((rows, cols), f32)] * 4,
            *[pltpu.VMEM((blocks + rows, 2 * cols), f32)] * 6,
            pltpu.VMEM((rows, 16, 8, cols), f32),
            pltpu.VMEM((rows, levels, levels), jnp.bfloat16),
            pltpu.VMEM((rows, levels, levels), jnp.bfloat16),
            pltpu.VMEM((rows, levels, cols), f32),
            dma,
            dma((6,)),
            dma((2, blocks)),
            dma((2, blocks)),
            dma((4,)),
            dma((4,)),
            dma((4,)),
            dma((4,)),
            dma((2, tracers)),
            dma((2, tracers)),
        ],
        compiler_params=pltpu.CompilerParams(collective_id=0, has_side_effects=True),
    )(dep_tile, dep_col, adjoint_in, frac_x, frac_y, jnp.swapaxes(block_inverse, 1, 2), coupling)


def solution(mesh):
    return jax.shard_map(
        on_device,
        mesh=mesh,
        in_specs=(
            P("lat", None, None, "lon"),
            P("lat", "lon"),
            P("lat", "lon"),
            P("lat"),
            P("lat"),
            P("lat", None, None, None),
            P("lat", "lon"),
        ),
        out_specs=P("lat", None, None, "lon"),
        check_vma=False,
    )
```

```python
import jax
import jax.numpy as jnp
from jax import lax
from jax.experimental import pallas as pl
from jax.experimental.pallas import tpu as pltpu
from jax.sharding import PartitionSpec as P

MESH = pl.DeviceIdType.MESH
ORDER = [(3, 0), (2, 0), (3, 1), (2, 1), (3, 2), (2, 2), (0, 0), (0, 1), (0, 2), (1, 0), (1, 1), (1, 2)]
HEAD, HEAD2 = 2, 4


def cubic(f):
    p, m1, m2 = f + 1.0, f - 1.0, f - 2.0
    sixth = 1.0 / 6.0
    return (-f * m1 * m2 * sixth, p * m1 * m2 * 0.5, -p * f * m2 * 0.5, p * f * m1 * sixth)


def kernel(
    tile_hbm, col_hbm, x_hbm, fx_hbm, fy_hbm, inv_hbm, cpl_hbm, out_ref,
    tile_ref, col_ref, fx_ref, fy_ref, inv_ref, cpl_ref, own, left, right, acc, from_prev, from_next, fxl, fxr, fyl, fyr,
    edge_r, edge_l, hop_l, hop_r, far_l, far_r, weights, ahi, alo, bcol,
    own_sem, in_sem, send_sem, recv_sem, fsend, frecv, esend, erecv, lsend, lrecv,
):
    rows, tracers, levels, cols = x_hbm.shape
    half = levels // 2
    nlon, nlat = lax.axis_size("lon"), lax.axis_size("lat")
    lon, lat = lax.axis_index("lon"), lax.axis_index("lat")
    to_right = (lat, lax.rem(lon + 1, nlon))
    to_left = (lat, lax.rem(lon + nlon - 1, nlon))
    has_prev, has_next = lat > 0, lat < nlat - 1

    barrier = pltpu.get_barrier_semaphore()
    pl.semaphore_signal(barrier, inc=1, device_id=to_right, device_id_type=MESH)
    pl.semaphore_signal(barrier, inc=1, device_id=to_left, device_id_type=MESH)

    @pl.when(has_prev)
    def _():
        pl.semaphore_signal(barrier, inc=1, device_id=(lat - 1, lon), device_id_type=MESH)

    @pl.when(has_next)
    def _():
        pl.semaphore_signal(barrier, inc=1, device_id=(lat + 1, lon), device_id_type=MESH)

    def remote(src, dst, ss, rs, to):
        return pltpu.make_async_remote_copy(src, dst, ss, rs, device_id=to, device_id_type=MESH)

    pl.semaphore_wait(barrier, 2 + has_prev.astype(jnp.int32) + has_next.astype(jnp.int32))

    edge_copies = [
        remote(edge_r, hop_l, esend.at[0], erecv.at[0], to_right),
        remote(edge_l, hop_r, esend.at[1], erecv.at[1], to_left),
        remote(hop_l, far_l, esend.at[2], erecv.at[2], to_right),
        remote(hop_r, far_r, esend.at[3], erecv.at[3], to_left),
    ]
    small = [
        remote(fx_hbm, fxl, fsend.at[0], frecv.at[0], to_right),
        remote(fy_hbm, fyl, fsend.at[1], frecv.at[1], to_right),
        remote(fx_hbm, fxr, fsend.at[2], frecv.at[2], to_left),
        remote(fy_hbm, fyr, fsend.at[3], frecv.at[3], to_left),
    ]
    big = []
    for k, (r, t) in enumerate(ORDER):
        big.append((
            remote(x_hbm.at[r, t], left.at[k], send_sem.at[0, k], recv_sem.at[0, k], to_right),
            remote(x_hbm.at[r, t], right.at[k], send_sem.at[1, k], recv_sem.at[1, k], to_left),
        ))
    for a, b in big[:HEAD]:
        a.start()
        b.start()
    for copy in small:
        copy.start()
    own_copy = pltpu.make_async_copy(x_hbm, own, own_sem)
    own_copy.start()
    loads = [
        pltpu.make_async_copy(src, dst, in_sem.at[i])
        for i, (src, dst) in enumerate((
            (fx_hbm, fx_ref), (fy_hbm, fy_ref), (tile_hbm, tile_ref),
            (col_hbm, col_ref), (cpl_hbm, cpl_ref), (inv_hbm, inv_ref),
        ))
    ]
    for copy in loads:
        copy.start()
    for copy in loads[:2]:
        copy.wait()

    own_copy.wait()
    eye = lax.broadcasted_iota(jnp.int32, (cols, cols), 0) == lax.broadcasted_iota(jnp.int32, (cols, cols), 1)
    rest = levels - cols
    eye_rest = lax.broadcasted_iota(jnp.int32, (rest, cols), 0) == lax.broadcasted_iota(jnp.int32, (rest, cols), 1)
    for r in range(rows):
        for t in range(tracers):
            k = r * tracers + t
            for lane, edge in ((cols - 1, edge_r), (0, edge_l)):
                column = jnp.broadcast_to(own[r, t, :, lane : lane + 1], (levels, cols))
                edge[k : k + 1, 0:cols] = jnp.sum(jnp.where(eye, column[:cols], 0.0), axis=0, keepdims=True)
                edge[k : k + 1, cols : 2 * cols] = jnp.sum(jnp.where(eye_rest, column[cols:], 0.0), axis=0, keepdims=True)
    base = rows * tracers
    for lane, edge in ((cols - 1, edge_r), (0, edge_l)):
        edge[base : base + rows, 0:cols] = jnp.broadcast_to(fx_ref[:, lane : lane + 1], (rows, cols))
        edge[base : base + rows, cols : 2 * cols] = jnp.broadcast_to(fy_ref[:, lane : lane + 1], (rows, cols))

    edge_copies[0].start()
    edge_copies[1].start()
    for a, b in big[HEAD:HEAD2]:
        a.start()
        b.start()
    for copy in loads[2:]:
        copy.wait()

    edge_copies[0].wait_recv()
    edge_copies[2].start()
    for a, _ in big[HEAD2:]:
        a.start()
    edge_copies[1].wait_recv()
    edge_copies[3].start()
    for _, b in big[HEAD2:]:
        b.start()

    sub = lax.broadcasted_iota(jnp.int32, (levels, cols), 0)
    for r in range(rows):
        top = jnp.concatenate([inv_ref[r, :, 0, :], jnp.zeros((half, half), jnp.float32)], axis=1)
        low = jnp.concatenate([jnp.zeros((half, half), jnp.float32), inv_ref[r, :, 1, :]], axis=1)
        whole = jnp.concatenate([top, low], axis=0)
        hi = whole.astype(jnp.bfloat16)
        ahi[r] = hi
        alo[r] = (whole - hi.astype(jnp.float32)).astype(jnp.bfloat16)
        column = jnp.concatenate([inv_ref[r, :, 0, half - 1 : half], inv_ref[r, :, 1, 0:1]], axis=0)
        bcol[r] = jnp.broadcast_to(column, (levels, cols))

    for copy in small:
        copy.wait_recv()
    edge_copies[2].wait_recv()
    edge_copies[3].wait_recv()

    lane = lax.broadcasted_iota(jnp.int32, (8, cols), 1)
    shifts = [tile_ref[r] * cols + col_ref[r] for r in range(rows)]

    def sources(s, b):
        d = s + (b - 1)
        return lax.shift_right_arithmetic(lane + d, 7), jnp.bitwise_and(d, cols - 1)

    def vec(ref, r, c0=0):
        return jnp.broadcast_to(ref[r : r + 1, c0 : c0 + cols], (8, cols))

    for r in range(rows):
        s = shifts[r]
        fx3 = (vec(fx_ref, r), vec(fxl, r), vec(fxr, r))
        fy3 = (vec(fy_ref, r), vec(fyl, r), vec(fyr, r))
        for b in range(4):
            where, turn = sources(s, b)
            shifted = []
            for (here, l, rt), c0 in ((fx3, 0), (fy3, cols)):
                v = jnp.where(where > 0, l, jnp.where(where < 0, rt, here))
                if b == 3:
                    v = jnp.where(where == 2, vec(far_l, base + r, c0), v)
                if b == 0:
                    v = jnp.where(where == -2, vec(far_r, base + r, c0), v)
                shifted.append(pltpu.roll(v, turn, 1))
            wx = cubic(shifted[0])[b]
            for a, wy in enumerate(cubic(shifted[1])):
                weights[r, a * 4 + b] = wx * wy

    lane8 = lane - lax.broadcasted_iota(jnp.int32, (8, cols), 0)

    def spread(k, r, t):
        s = shifts[r]
        sv = jnp.full((8, cols), 0, jnp.int32) + s
        lo_right, hi_left = sv <= 0, sv >= -1
        src = [sources(s, b) for b in range(4)]
        g = [[weights[r, a * 4 + b] for b in range(4)] for a in range(4)]
        kk = r * tracers + t
        for i in range(levels // 8):
            rs = slice(8 * i, 8 * i + 8)
            here, l, rt = own[r, t, rs, :], left[k, rs, :], right[k, rs, :]
            c0 = cols * ((8 * i) // cols)
            far = jnp.where(hi_left, vec(far_l, kk, c0), vec(far_r, kk, c0))
            far = jnp.sum(jnp.where(lane8 == (8 * i) % cols, far, 0.0), axis=1, keepdims=True)
            far = jnp.broadcast_to(far, (8, cols))
            near_lo, near_hi = jnp.where(lo_right, rt, l), jnp.where(hi_left, l, rt)
            u = []
            for b in range(4):
                where, turn = src[b]
                v = jnp.where(where == 0, here, near_lo if b < 2 else near_hi)
                if b == 3:
                    v = jnp.where(where == 2, far, v)
                if b == 0:
                    v = jnp.where(where == -2, far, v)
                u.append(pltpu.roll(v, turn, 1))
            for a in range(4):
                part = (g[a][0] * u[0] + g[a][1] * u[1]) + (g[a][2] * u[2] + g[a][3] * u[3])
                first = r == 3 or (r == 2 and a == 0) or (r == 0 and a < 2)
                acc[t, r + a, rs, :] = part if first else acc[t, r + a, rs, :] + part

    def next_copy(t):
        return remote(acc.at[t, pl.ds(rows + 1, 2)], from_prev.at[t], lsend.at[0, t], lrecv.at[0, t], (lat + 1, lon))

    def prev_copy(t):
        return remote(acc.at[t, 0], from_next.at[t], lsend.at[1, t], lrecv.at[1, t], (lat - 1, lon))

    def final(t):
        @pl.when(has_prev)
        def _():
            next_copy(t).wait_recv()

        @pl.when(has_next)
        def _():
            prev_copy(t).wait_recv()

        for i in range(rows):
            x = acc[t, i + 1]
            if i < 2:
                x = x + from_prev[t, i]
            if i == rows - 1:
                x = x + from_next[t]
            hi = x.astype(jnp.bfloat16)
            lo = (x - hi.astype(jnp.float32)).astype(jnp.bfloat16)
            p = jnp.dot(ahi[i], hi, preferred_element_type=jnp.float32)
            p = p + jnp.dot(ahi[i], lo, preferred_element_type=jnp.float32)
            p = p + jnp.dot(alo[i], hi, preferred_element_type=jnp.float32)
            c = cpl_ref[i : i + 1, :]
            above = jnp.broadcast_to(c * p[half : half + 1], (levels, cols))
            below = jnp.broadcast_to(c * p[half - 1 : half], (levels, cols))
            out_ref[i, t] = p + bcol[i] * jnp.where(sub < half, above, below)

    @pl.when(jnp.logical_not(has_prev))
    def _():
        from_prev[...] = jnp.zeros_like(from_prev)

    @pl.when(jnp.logical_not(has_next))
    def _():
        from_next[...] = jnp.zeros_like(from_next)

    for k, (r, t) in enumerate(ORDER):
        big[k][0].wait_recv()
        big[k][1].wait_recv()
        spread(k, r, t)
        if r == 2:
            @pl.when(has_next)
            def _(t=t):
                next_copy(t).start()

        if r == 0:
            @pl.when(has_prev)
            def _(t=t):
                prev_copy(t).start()

        if r == 1:
            final(t)

    for copy in small + edge_copies:
        copy.wait_send()
    for a, b in big:
        a.wait_send()
        b.wait_send()

    @pl.when(has_next)
    def _():
        for t in range(tracers):
            next_copy(t).wait_send()

    @pl.when(has_prev)
    def _():
        for t in range(tracers):
            prev_copy(t).wait_send()


def on_device(adjoint_in, frac_x, frac_y, dep_tile, dep_col, block_inverse, coupling):
    rows, tracers, levels, cols = adjoint_in.shape
    blocks = rows * tracers
    f32, dma = jnp.float32, pltpu.SemaphoreType.DMA
    return pl.pallas_call(
        kernel,
        out_shape=pltpu.VMEM(adjoint_in.shape, f32),
        in_specs=[pl.BlockSpec(memory_space=pl.ANY)] * 7,
        out_specs=pl.BlockSpec(memory_space=pltpu.VMEM),
        scratch_shapes=[
            pltpu.SMEM(dep_tile.shape, jnp.int32),
            pltpu.SMEM(dep_col.shape, jnp.int32),
            pltpu.VMEM((rows, cols), f32),
            pltpu.VMEM((rows, cols), f32),
            pltpu.VMEM((rows, levels // 2, 2, levels // 2), f32),
            pltpu.VMEM((rows, cols), f32),
            pltpu.VMEM((rows, tracers, levels, cols), f32),
            pltpu.VMEM((blocks, levels, cols), f32),
            pltpu.VMEM((blocks, levels, cols), f32),
            pltpu.VMEM((tracers, rows + 3, levels, cols), f32),
            pltpu.VMEM((tracers, 2, levels, cols), f32),
            pltpu.VMEM((tracers, levels, cols), f32),
            *[pltpu.VMEM((rows, cols), f32)] * 4,
            *[pltpu.VMEM((blocks + rows, 2 * cols), f32)] * 6,
            pltpu.VMEM((rows, 16, 8, cols), f32),
            pltpu.VMEM((rows, levels, levels), jnp.bfloat16),
            pltpu.VMEM((rows, levels, levels), jnp.bfloat16),
            pltpu.VMEM((rows, levels, cols), f32),
            dma,
            dma((6,)),
            dma((2, blocks)),
            dma((2, blocks)),
            dma((4,)),
            dma((4,)),
            dma((4,)),
            dma((4,)),
            dma((2, tracers)),
            dma((2, tracers)),
        ],
        compiler_params=pltpu.CompilerParams(collective_id=0, has_side_effects=True),
    )(dep_tile, dep_col, adjoint_in, frac_x, frac_y, jnp.swapaxes(block_inverse, 1, 2), coupling)


def solution(mesh):
    return jax.shard_map(
        on_device,
        mesh=mesh,
        in_specs=(
            P("lat", None, None, "lon"),
            P("lat", "lon"),
            P("lat", "lon"),
            P("lat"),
            P("lat"),
            P("lat", None, None, None),
            P("lat", "lon"),
        ),
        out_specs=P("lat", None, None, "lon"),
        check_vma=False,
    )
```

```python
import jax
import jax.numpy as jnp
from jax import lax
from jax.experimental import pallas as pl
from jax.experimental.pallas import tpu as pltpu
from jax.sharding import PartitionSpec as P

MESH = pl.DeviceIdType.MESH
ORDER = [(0, 0), (0, 1), (0, 2), (3, 0), (2, 0), (3, 1), (2, 1), (3, 2), (2, 2), (1, 0), (1, 1), (1, 2)]
HEAD, HEAD2 = 2, 4


def cubic(f):
    p, m1, m2 = f + 1.0, f - 1.0, f - 2.0
    sixth = 1.0 / 6.0
    return (-f * m1 * m2 * sixth, p * m1 * m2 * 0.5, -p * f * m2 * 0.5, p * f * m1 * sixth)


def kernel(
    tile_hbm, col_hbm, x_hbm, fx_hbm, fy_hbm, inv_hbm, cpl_hbm, out_ref,
    tile_ref, col_ref, fx_ref, fy_ref, inv_ref, cpl_ref, own, left, right, acc, from_prev, from_next, fxl, fxr, fyl, fyr,
    edge_r, edge_l, hop_l, hop_r, far_l, far_r, weights, ahi, alo, bcol,
    own_sem, in_sem, send_sem, recv_sem, fsend, frecv, esend, erecv, lsend, lrecv,
):
    rows, tracers, levels, cols = x_hbm.shape
    half = levels // 2
    nlon, nlat = lax.axis_size("lon"), lax.axis_size("lat")
    lon, lat = lax.axis_index("lon"), lax.axis_index("lat")
    to_right = (lat, lax.rem(lon + 1, nlon))
    to_left = (lat, lax.rem(lon + nlon - 1, nlon))
    has_prev, has_next = lat > 0, lat < nlat - 1

    barrier = pltpu.get_barrier_semaphore()
    pl.semaphore_signal(barrier, inc=1, device_id=to_right, device_id_type=MESH)
    pl.semaphore_signal(barrier, inc=1, device_id=to_left, device_id_type=MESH)

    @pl.when(has_prev)
    def _():
        pl.semaphore_signal(barrier, inc=1, device_id=(lat - 1, lon), device_id_type=MESH)

    @pl.when(has_next)
    def _():
        pl.semaphore_signal(barrier, inc=1, device_id=(lat + 1, lon), device_id_type=MESH)

    def remote(src, dst, ss, rs, to):
        return pltpu.make_async_remote_copy(src, dst, ss, rs, device_id=to, device_id_type=MESH)

    pl.semaphore_wait(barrier, 2 + has_prev.astype(jnp.int32) + has_next.astype(jnp.int32))

    edge_copies = [
        remote(edge_r, hop_l, esend.at[0], erecv.at[0], to_right),
        remote(edge_l, hop_r, esend.at[1], erecv.at[1], to_left),
        remote(hop_l, far_l, esend.at[2], erecv.at[2], to_right),
        remote(hop_r, far_r, esend.at[3], erecv.at[3], to_left),
    ]
    small = [
        remote(fx_hbm, fxl, fsend.at[0], frecv.at[0], to_right),
        remote(fy_hbm, fyl, fsend.at[1], frecv.at[1], to_right),
        remote(fx_hbm, fxr, fsend.at[2], frecv.at[2], to_left),
        remote(fy_hbm, fyr, fsend.at[3], frecv.at[3], to_left),
    ]
    big = []
    for k, (r, t) in enumerate(ORDER):
        big.append((
            remote(x_hbm.at[r, t], left.at[k], send_sem.at[0, k], recv_sem.at[0, k], to_right),
            remote(x_hbm.at[r, t], right.at[k], send_sem.at[1, k], recv_sem.at[1, k], to_left),
        ))
    for a, b in big[:HEAD]:
        a.start()
        b.start()
    for copy in small:
        copy.start()
    own_copy = pltpu.make_async_copy(x_hbm, own, own_sem)
    own_copy.start()
    loads = [
        pltpu.make_async_copy(src, dst, in_sem.at[i])
        for i, (src, dst) in enumerate((
            (fx_hbm, fx_ref), (fy_hbm, fy_ref), (tile_hbm, tile_ref),
            (col_hbm, col_ref), (cpl_hbm, cpl_ref), (inv_hbm, inv_ref),
        ))
    ]
    for copy in loads:
        copy.start()
    for copy in loads[:2]:
        copy.wait()

    own_copy.wait()
    eye = lax.broadcasted_iota(jnp.int32, (cols, cols), 0) == lax.broadcasted_iota(jnp.int32, (cols, cols), 1)
    rest = levels - cols
    eye_rest = lax.broadcasted_iota(jnp.int32, (rest, cols), 0) == lax.broadcasted_iota(jnp.int32, (rest, cols), 1)
    for r in range(rows):
        for t in range(tracers):
            k = r * tracers + t
            for lane, edge in ((cols - 1, edge_r), (0, edge_l)):
                column = jnp.broadcast_to(own[r, t, :, lane : lane + 1], (levels, cols))
                edge[k : k + 1, 0:cols] = jnp.sum(jnp.where(eye, column[:cols], 0.0), axis=0, keepdims=True)
                edge[k : k + 1, cols : 2 * cols] = jnp.sum(jnp.where(eye_rest, column[cols:], 0.0), axis=0, keepdims=True)
    base = rows * tracers
    for lane, edge in ((cols - 1, edge_r), (0, edge_l)):
        edge[base : base + rows, 0:cols] = jnp.broadcast_to(fx_ref[:, lane : lane + 1], (rows, cols))
        edge[base : base + rows, cols : 2 * cols] = jnp.broadcast_to(fy_ref[:, lane : lane + 1], (rows, cols))

    edge_copies[0].start()
    edge_copies[1].start()
    for a, b in big[HEAD:HEAD2]:
        a.start()
        b.start()
    for copy in loads[2:]:
        copy.wait()

    edge_copies[0].wait_recv()
    edge_copies[2].start()
    for a, _ in big[HEAD2:]:
        a.start()
    edge_copies[1].wait_recv()
    edge_copies[3].start()
    for _, b in big[HEAD2:]:
        b.start()

    sub = lax.broadcasted_iota(jnp.int32, (levels, cols), 0)
    for r in range(rows):
        top = jnp.concatenate([inv_ref[r, :, 0, :], jnp.zeros((half, half), jnp.float32)], axis=1)
        low = jnp.concatenate([jnp.zeros((half, half), jnp.float32), inv_ref[r, :, 1, :]], axis=1)
        whole = jnp.concatenate([top, low], axis=0)
        hi = whole.astype(jnp.bfloat16)
        ahi[r] = hi
        alo[r] = (whole - hi.astype(jnp.float32)).astype(jnp.bfloat16)
        column = jnp.concatenate([inv_ref[r, :, 0, half - 1 : half], inv_ref[r, :, 1, 0:1]], axis=0)
        bcol[r] = jnp.broadcast_to(column, (levels, cols))

    for copy in small:
        copy.wait_recv()
    edge_copies[2].wait_recv()
    edge_copies[3].wait_recv()

    lane = lax.broadcasted_iota(jnp.int32, (8, cols), 1)
    shifts = [tile_ref[r] * cols + col_ref[r] for r in range(rows)]

    def sources(s, b):
        d = s + (b - 1)
        return lax.shift_right_arithmetic(lane + d, 7), jnp.bitwise_and(d, cols - 1)

    def vec(ref, r, c0=0):
        return jnp.broadcast_to(ref[r : r + 1, c0 : c0 + cols], (8, cols))

    for r in range(rows):
        s = shifts[r]
        fx3 = (vec(fx_ref, r), vec(fxl, r), vec(fxr, r))
        fy3 = (vec(fy_ref, r), vec(fyl, r), vec(fyr, r))
        for b in range(4):
            where, turn = sources(s, b)
            shifted = []
            for (here, l, rt), c0 in ((fx3, 0), (fy3, cols)):
                v = jnp.where(where > 0, l, jnp.where(where < 0, rt, here))
                if b == 3:
                    v = jnp.where(where == 2, vec(far_l, base + r, c0), v)
                if b == 0:
                    v = jnp.where(where == -2, vec(far_r, base + r, c0), v)
                shifted.append(pltpu.roll(v, turn, 1))
            wx = cubic(shifted[0])[b]
            for a, wy in enumerate(cubic(shifted[1])):
                weights[r, a * 4 + b] = wx * wy

    lane8 = lane - lax.broadcasted_iota(jnp.int32, (8, cols), 0)

    def spread(k, r, t):
        s = shifts[r]
        sv = jnp.full((8, cols), 0, jnp.int32) + s
        lo_right, hi_left = sv <= 0, sv >= -1
        src = [sources(s, b) for b in range(4)]
        g = [[weights[r, a * 4 + b] for b in range(4)] for a in range(4)]
        kk = r * tracers + t
        for i in range(levels // 8):
            rs = slice(8 * i, 8 * i + 8)
            here, l, rt = own[r, t, rs, :], left[k, rs, :], right[k, rs, :]
            c0 = cols * ((8 * i) // cols)
            far = jnp.where(hi_left, vec(far_l, kk, c0), vec(far_r, kk, c0))
            far = jnp.sum(jnp.where(lane8 == (8 * i) % cols, far, 0.0), axis=1, keepdims=True)
            far = jnp.broadcast_to(far, (8, cols))
            near_lo, near_hi = jnp.where(lo_right, rt, l), jnp.where(hi_left, l, rt)
            u = []
            for b in range(4):
                where, turn = src[b]
                v = jnp.where(where == 0, here, near_lo if b < 2 else near_hi)
                if b == 3:
                    v = jnp.where(where == 2, far, v)
                if b == 0:
                    v = jnp.where(where == -2, far, v)
                u.append(pltpu.roll(v, turn, 1))
            for a in range(4):
                part = (g[a][0] * u[0] + g[a][1] * u[1]) + (g[a][2] * u[2] + g[a][3] * u[3])
                first = r == 0 or (r == 3 and a > 0)
                acc[t, r + a, rs, :] = part if first else acc[t, r + a, rs, :] + part

    def next_copy(t):
        return remote(acc.at[t, pl.ds(rows + 1, 2)], from_prev.at[t], lsend.at[0, t], lrecv.at[0, t], (lat + 1, lon))

    def prev_copy(t):
        return remote(acc.at[t, 0], from_next.at[t], lsend.at[1, t], lrecv.at[1, t], (lat - 1, lon))

    def final(t):
        @pl.when(has_prev)
        def _():
            next_copy(t).wait_recv()

        @pl.when(has_next)
        def _():
            prev_copy(t).wait_recv()

        for i in range(rows):
            x = acc[t, i + 1]
            if i < 2:
                x = x + from_prev[t, i]
            if i == rows - 1:
                x = x + from_next[t]
            hi = x.astype(jnp.bfloat16)
            lo = (x - hi.astype(jnp.float32)).astype(jnp.bfloat16)
            p = jnp.dot(ahi[i], hi, preferred_element_type=jnp.float32)
            p = p + jnp.dot(ahi[i], lo, preferred_element_type=jnp.float32)
            p = p + jnp.dot(alo[i], hi, preferred_element_type=jnp.float32)
            c = cpl_ref[i : i + 1, :]
            above = jnp.broadcast_to(c * p[half : half + 1], (levels, cols))
            below = jnp.broadcast_to(c * p[half - 1 : half], (levels, cols))
            out_ref[i, t] = p + bcol[i] * jnp.where(sub < half, above, below)

    @pl.when(jnp.logical_not(has_prev))
    def _():
        from_prev[...] = jnp.zeros_like(from_prev)

    @pl.when(jnp.logical_not(has_next))
    def _():
        from_next[...] = jnp.zeros_like(from_next)

    for k, (r, t) in enumerate(ORDER):
        big[k][0].wait_recv()
        big[k][1].wait_recv()
        spread(k, r, t)
        if r == 2:
            @pl.when(has_next)
            def _(t=t):
                next_copy(t).start()

        if r == 0:
            @pl.when(has_prev)
            def _(t=t):
                prev_copy(t).start()

        if r == 1:
            final(t)

    for copy in small + edge_copies:
        copy.wait_send()
    for a, b in big:
        a.wait_send()
        b.wait_send()

    @pl.when(has_next)
    def _():
        for t in range(tracers):
            next_copy(t).wait_send()

    @pl.when(has_prev)
    def _():
        for t in range(tracers):
            prev_copy(t).wait_send()


def on_device(adjoint_in, frac_x, frac_y, dep_tile, dep_col, block_inverse, coupling):
    rows, tracers, levels, cols = adjoint_in.shape
    blocks = rows * tracers
    f32, dma = jnp.float32, pltpu.SemaphoreType.DMA
    return pl.pallas_call(
        kernel,
        out_shape=pltpu.VMEM(adjoint_in.shape, f32),
        in_specs=[pl.BlockSpec(memory_space=pl.ANY)] * 7,
        out_specs=pl.BlockSpec(memory_space=pltpu.VMEM),
        scratch_shapes=[
            pltpu.SMEM(dep_tile.shape, jnp.int32),
            pltpu.SMEM(dep_col.shape, jnp.int32),
            pltpu.VMEM((rows, cols), f32),
            pltpu.VMEM((rows, cols), f32),
            pltpu.VMEM((rows, levels // 2, 2, levels // 2), f32),
            pltpu.VMEM((rows, cols), f32),
            pltpu.VMEM((rows, tracers, levels, cols), f32),
            pltpu.VMEM((blocks, levels, cols), f32),
            pltpu.VMEM((blocks, levels, cols), f32),
            pltpu.VMEM((tracers, rows + 3, levels, cols), f32),
            pltpu.VMEM((tracers, 2, levels, cols), f32),
            pltpu.VMEM((tracers, levels, cols), f32),
            *[pltpu.VMEM((rows, cols), f32)] * 4,
            *[pltpu.VMEM((blocks + rows, 2 * cols), f32)] * 6,
            pltpu.VMEM((rows, 16, 8, cols), f32),
            pltpu.VMEM((rows, levels, levels), jnp.bfloat16),
            pltpu.VMEM((rows, levels, levels), jnp.bfloat16),
            pltpu.VMEM((rows, levels, cols), f32),
            dma,
            dma((6,)),
            dma((2, blocks)),
            dma((2, blocks)),
            dma((4,)),
            dma((4,)),
            dma((4,)),
            dma((4,)),
            dma((2, tracers)),
            dma((2, tracers)),
        ],
        compiler_params=pltpu.CompilerParams(collective_id=0, has_side_effects=True),
    )(dep_tile, dep_col, adjoint_in, frac_x, frac_y, jnp.swapaxes(block_inverse, 1, 2), coupling)


def solution(mesh):
    return jax.shard_map(
        on_device,
        mesh=mesh,
        in_specs=(
            P("lat", None, None, "lon"),
            P("lat", "lon"),
            P("lat", "lon"),
            P("lat"),
            P("lat"),
            P("lat", None, None, None),
            P("lat", "lon"),
        ),
        out_specs=P("lat", None, None, "lon"),
        check_vma=False,
    )
```
